32 devices in a mesh: gx: 8 (over z, y), ha: 4 (over x, core).
Axes of the slice: x: 2, y: 2, z: 4, core: 2. Of those that a mesh axis runs over, the one named last changes fastest.
Arguments:
- value_field: float32 [8, 32, 16, 16], P('ha', None, 'gx'), may hold values from -6 to 6
- avoid_field: float32 [8, 32, 16, 16], P('ha', None, 'gx'), may hold values from -6 to 6
- sample_adjoint: float32 [8, 4, 8, 128], P('gx', 'ha'), may hold values from -6 to 6
- offset_y: float32 [8, 4, 8, 128], P('gx', 'ha'), may hold values from 0 to 1
- offset_s: float32 [8, 4, 8, 128], P('gx', 'ha'), may hold values from 0 to 1
- start_xy: int32 [8, 4, 8, 128], P('gx', 'ha'), may hold values from 0 to 30, as said below
- start_hs: int32 [8, 4, 8, 128], P('gx', 'ha'), may hold values from 0 to 62, as said below
- send_counts: int32 [8, 4, 8], P('gx', 'ha'), may hold values from 16 to 128, as said below
Outputs:
- next_value: float32 [8, 32, 16, 16], P('ha', None, 'gx')
- value_grad: float32 [8, 32, 16, 16], P('ha', None, 'gx')
- avoid_grad: float32 [8, 32, 16, 16], P('ha', None, 'gx')
The draws below stay inside these ranges and needn't reach their ends.
Inputs may be any that keep to these rules, and one draw needn't show every extreme that they name: `start_xy`: the y cell of a start is at most 14. `start_hs`: the speed cell of a start is at most 30. `send_counts`: the live slots of a row are its first ones. For each index along ha, one owner drawn from the seed gets all 128 slots live from every sender.
All inputs are finite; a program needn't handle non-finite values.
Results may differ from the reference program's by a relative error of at most 0.00002.
Values sent between devices are 32-bit elements; how exact they have to be, the bound alone decides.
A program may use at most 64 MiB of HBM per device.

```python
import math
import jax
import jax.numpy as jnp
from jax import lax

CX = 2
CH = 2
NS = 32
CAP = 128
ROWGROUPS = 8
HEADGROUPS = 4
NX = 16
NY = 16
NH = 8


def draw_start_xy(key, part):
    first_key, second_key = jax.random.split(jax.random.fold_in(key, 11))
    shape_all = (ROWGROUPS, HEADGROUPS, ROWGROUPS, CAP)
    row_cells = jax.random.randint(first_key, shape_all, 0, CX)
    col_cells = jax.random.randint(second_key, shape_all, 0, NY - 1)
    return (row_cells * NY + col_cells).astype(jnp.int32)


def draw_start_hs(key, part):
    first_key, second_key = jax.random.split(jax.random.fold_in(key, 23))
    shape_all = (ROWGROUPS, HEADGROUPS, ROWGROUPS, CAP)
    head_cells = jax.random.randint(first_key, shape_all, 0, CH)
    speed_cells = jax.random.randint(second_key, shape_all, 0, NS - 1)
    return (head_cells * NS + speed_cells).astype(jnp.int32)


def draw_send_counts(key, part):
    first_key, second_key = jax.random.split(jax.random.fold_in(key, 37))
    shape_all = (ROWGROUPS, HEADGROUPS, ROWGROUPS)
    counts = jax.random.randint(first_key, shape_all, CAP // 8, 3 * CAP // 4 + 1)
    busiest = jax.random.randint(second_key, (HEADGROUPS,), 0, ROWGROUPS)
    owner_index = jnp.arange(ROWGROUPS, dtype=jnp.int32)[None, None, :]
    filled = owner_index == busiest[None, :, None]
    return jnp.where(filled, CAP, counts).astype(jnp.int32)


def shard_levels(stream_key, extent, cuts, least, high):
    def one(dim, shards_of):
        steps = jax.random.uniform(jax.random.fold_in(jax.random.fold_in(stream_key, 6), dim), (shards_of,), jnp.float32, least / len(cuts), high / len(cuts))
        return jnp.repeat(jnp.exp(steps), extent[dim] // shards_of).reshape((-1,) + (1,) * (len(extent) - dim - 1))

    factor_of = one(*cuts[0])
    for cut in cuts[1:]:
        factor_of = factor_of * one(*cut)
    return factor_of


def noise(key, shape, scale, reach, cuts=(), held_as=jnp.bfloat16):
    loudness = shard_levels(key, shape, cuts, -0.22, 0.18) if cuts else 1.0
    array = jax.random.normal(key, shape, jnp.float32) * scale * loudness
    return jnp.minimum(jnp.maximum(array, -reach), reach).astype(held_as)


def setup_inputs(seed: int = 0) -> dict:
    streams_of = jax.random.split(jax.random.key(seed), 9)
    value_field = noise(streams_of[0], (NH, NS, NX, NY), 1.0, 6.0, ((0, 4), (2, 8)), jnp.float32)
    avoid_field = noise(streams_of[1], (NH, NS, NX, NY), 1.0, 6.0, ((0, 4), (2, 8)), jnp.float32)
    sample_adjoint = noise(streams_of[2], (ROWGROUPS, HEADGROUPS, ROWGROUPS, CAP), 1.0, 6.0, ((0, 8), (1, 4)), jnp.float32)
    offset_y = jnp.clip(1.0 * jax.random.uniform(streams_of[3], (ROWGROUPS, HEADGROUPS, ROWGROUPS, CAP), jnp.float32) ** shard_levels(streams_of[3], (ROWGROUPS, HEADGROUPS, ROWGROUPS, CAP), ((0, 8), (1, 4)), -0.2, 0.2), 0.0, 1.0)
    offset_s = jnp.clip(1.0 * jax.random.uniform(streams_of[4], (ROWGROUPS, HEADGROUPS, ROWGROUPS, CAP), jnp.float32) ** shard_levels(streams_of[4], (ROWGROUPS, HEADGROUPS, ROWGROUPS, CAP), ((0, 8), (1, 4)), -0.2, 0.2), 0.0, 1.0)
    start_xy = draw_start_xy(jax.random.fold_in(streams_of[8], 71), 0)
    start_hs = draw_start_hs(jax.random.fold_in(streams_of[8], 71), 0)
    send_counts = draw_send_counts(jax.random.fold_in(streams_of[8], 71), 0)
    return dict(value_field=value_field, avoid_field=avoid_field, sample_adjoint=sample_adjoint, offset_y=offset_y, offset_s=offset_s, start_xy=start_xy, start_hs=start_hs, send_counts=send_counts)


TIME_STEP = 0.3
SHARPNESS = 2.0
SOFTENING = 0.1
TURN_RATE = 0.5
ACCELERATION = 0.3
SLOWEST = 0.2
SPEED_RANGE = 0.8
FASTEST = 1.0

def smooth_abs(slope_value):
    return jnp.sqrt(slope_value * slope_value + SOFTENING * SOFTENING)

def edge_neighbours(grid_field, along_dim):
    length = grid_field.shape[along_dim]
    first_plane = lax.slice_in_dim(grid_field, 0, 1, axis=along_dim)
    last_plane = lax.slice_in_dim(grid_field, length - 1, length, axis=along_dim)
    upper_cells = jnp.concatenate([lax.slice_in_dim(grid_field, 1, length, axis=along_dim), last_plane], along_dim)
    lower_cells = jnp.concatenate([first_plane, lax.slice_in_dim(grid_field, 0, length - 1, axis=along_dim)], along_dim)
    return (upper_cells, lower_cells)

def linear_term(grid_field, upper_cells, lower_cells, factor):
    return factor * (upper_cells - lower_cells) * 0.5 - FASTEST * (upper_cells - 2.0 * grid_field + lower_cells) * 0.5

def turn_term(grid_field, upper_cells, lower_cells, turn_rate):
    return turn_rate * smooth_abs(0.5 * (upper_cells - lower_cells)) - turn_rate * 0.5 * (upper_cells - 2.0 * grid_field + lower_cells)

def coefficients(head_index, total_heads):
    heading_angle = 2.0 * math.pi / total_heads * head_index.astype(jnp.float32)
    speed_cell = SLOWEST + SPEED_RANGE * jnp.arange(NS, dtype=jnp.int32).astype(jnp.float32) / (NS - 1)
    along_x = jnp.cos(heading_angle)[:, None, None, None] * speed_cell[None, :, None, None]
    along_y = jnp.sin(heading_angle)[:, None, None, None] * speed_cell[None, :, None, None]
    return (along_x, along_y)

def hamilton_of(grid_field):
    along_x, along_y = coefficients(jnp.arange(NH, dtype=jnp.int32), NH)
    upper_cells, lower_cells = edge_neighbours(grid_field, 2)
    summed = linear_term(grid_field, upper_cells, lower_cells, along_x)
    upper_cells, lower_cells = edge_neighbours(grid_field, 3)
    summed = summed + linear_term(grid_field, upper_cells, lower_cells, along_y)
    upper_cells = jnp.roll(grid_field, -1, 0)
    lower_cells = jnp.roll(grid_field, 1, 0)
    summed = summed + turn_term(grid_field, upper_cells, lower_cells, TURN_RATE)
    upper_cells, lower_cells = edge_neighbours(grid_field, 1)
    return summed + turn_term(grid_field, upper_cells, lower_cells, ACCELERATION)

def step_map(value_field, avoid_field):
    relaxed = value_field - TIME_STEP * hamilton_of(value_field)
    return avoid_field + jax.nn.softplus(SHARPNESS * (relaxed - avoid_field)) / SHARPNESS

def reference(value_field, avoid_field, sample_adjoint, offset_y, offset_s, start_xy, start_hs, send_counts):
    slot_index = jnp.arange(CAP, dtype=jnp.int32)
    live_slot = slot_index[None, None, None, :] < send_counts[..., None]
    weight = jnp.where(live_slot, sample_adjoint, jnp.zeros_like(sample_adjoint))
    owner_index = jnp.arange(ROWGROUPS, dtype=jnp.int32)[None, None, :, None]
    block_index = jnp.arange(HEADGROUPS, dtype=jnp.int32)[None, :, None, None]
    x_cell = (owner_index * CX + start_xy // NY).astype(jnp.int32)
    y_cell = (start_xy % NY).astype(jnp.int32)
    h_cell = (block_index * CH + start_hs // NS).astype(jnp.int32)
    s_cell = (start_hs % NS).astype(jnp.int32)
    flat_index = (((h_cell * NS + s_cell) * NX + x_cell) * NY + y_cell).astype(jnp.int32).reshape(-1)
    plane = NX * NY
    deposited = jnp.zeros((NH * NS * NX * NY,), jnp.float32)
    deposited = deposited.at[flat_index].add((weight * (1.0 - offset_y) * (1.0 - offset_s)).reshape(-1))
    deposited = deposited.at[flat_index + 1].add((weight * offset_y * (1.0 - offset_s)).reshape(-1))
    deposited = deposited.at[flat_index + plane].add((weight * (1.0 - offset_y) * offset_s).reshape(-1))
    deposited = deposited.at[flat_index + plane + 1].add((weight * offset_y * offset_s).reshape(-1))
    deposited = deposited.reshape(NH, NS, NX, NY)
    next_value, pullback = jax.vjp(step_map, value_field, avoid_field)
    value_grad, avoid_grad = pullback(deposited)
    return (next_value, value_grad, avoid_grad)
```

```python
import functools
import math

import jax
import jax.numpy as jnp
import numpy as np
from jax import lax
from jax.experimental import pallas as pl
from jax.experimental.pallas import tpu as pltpu
from jax.sharding import PartitionSpec as P

TIME_STEP = 0.3
SHARPNESS = 2.0
SOFTENING = 0.1
TURN_RATE = 0.5
ACCELERATION = 0.3
SLOWEST = 0.2
SPEED_RANGE = 0.8
ROWS = 8
MESH = pl.DeviceIdType.MESH


def smooth_abs(slope):
    return jnp.sqrt(slope * slope + SOFTENING * SOFTENING)


def upper(plane, axis):
    n = plane.shape[axis]
    return jnp.concatenate(
        [lax.slice_in_dim(plane, 1, n, axis=axis), lax.slice_in_dim(plane, n - 1, n, axis=axis)], axis
    )


def lower(plane, axis):
    n = plane.shape[axis]
    return jnp.concatenate(
        [lax.slice_in_dim(plane, 0, 1, axis=axis), lax.slice_in_dim(plane, 0, n - 1, axis=axis)], axis
    )


def spread(up, down, axis):
    n = up.shape[axis]
    from_lower = jnp.concatenate(
        [lax.slice_in_dim(down, 0, 1, axis=axis), lax.slice_in_dim(up, 0, n - 1, axis=axis)], axis
    )
    from_upper = jnp.concatenate(
        [lax.slice_in_dim(down, 1, n, axis=axis), lax.slice_in_dim(up, n - 1, n, axis=axis)], axis
    )
    return from_lower + from_upper


def pick(table, index):
    chosen = jnp.float32(table[0])
    for i in range(1, len(table)):
        chosen = jnp.where(index == i, jnp.float32(table[i]), chosen)
    return chosen


def kernel(
    groups, blocks,
    value_h, avoid_h, weight_h, offy_h, offs_h, xy_h, hs_h, count_h,
    next_o, vgrad_o, agrad_o,
    value, avoid, weight, offy, offs, xy, hs, count,
    pay, got, xhalo, hhalo, carried, turned, cxhalo, chhalo,
    in_sem, pay_send, pay_recv, x_send, x_recv, h_send, h_recv,
    cx_send, cx_recv, ch_send, ch_recv, self_sem,
):
    heads, cells, lines, speeds = value.shape
    slots = weight.shape[1]
    me = lax.axis_index("gx")
    hb = lax.axis_index("ha")
    h_next = lax.rem(hb + 1, blocks)
    h_prev = lax.rem(hb + blocks - 1, blocks)
    has_prev = me > 0
    has_next = me < groups - 1

    barrier = pltpu.get_barrier_semaphore()

    def greet(d):
        pl.semaphore_signal(
            barrier, inc=1, device_id=(lax.rem(me + d, groups), hb), device_id_type=MESH
        )

    if groups <= 8:
        for d in range(1, groups):
            greet(d)
    else:
        pl.loop(1, groups)(greet)
    for other in (h_prev, h_next):
        pl.semaphore_signal(barrier, inc=1, device_id=(me, other), device_id_type=MESH)

    pairs = (
        (weight_h, weight), (offy_h, offy), (offs_h, offs), (xy_h, xy), (hs_h, hs), (count_h, count),
        (value_h, value), (avoid_h, avoid),
    )
    loads = [pltpu.make_async_copy(a, b, in_sem.at[i]) for i, (a, b) in enumerate(pairs)]
    for load in loads:
        load.start()
    for load in loads[:6]:
        load.wait()

    owners = lax.broadcasted_iota(jnp.int32, (groups, groups), 0)
    lanes = lax.broadcasted_iota(jnp.int32, (groups, groups), 1)
    live = jnp.sum(
        jnp.where(owners == lanes, jnp.broadcast_to(count[...], (groups, groups)), 0).astype(jnp.float32),
        axis=1, keepdims=True,
    )
    slot = lax.broadcasted_iota(jnp.int32, (groups, slots), 1).astype(jnp.float32)
    w = jnp.where(slot < live, weight[...], 0.0)
    oy = offy[...]
    os = offs[...]
    state = hs[...]
    head = lax.div(state, speeds)
    pay[:, 0, :] = w * (1.0 - oy)
    pay[:, 1, :] = w * oy
    pay[:, 2, :] = 1.0 - os
    pay[:, 3, :] = os
    pay[:, 4, :] = (head * (cells * lines) + xy[...]).astype(jnp.float32)
    pay[:, 5, :] = (state - head * speeds).astype(jnp.float32)
    pay[:, 6, :] = jnp.zeros((groups, slots), jnp.float32)
    pay[:, 7, :] = jnp.zeros((groups, slots), jnp.float32)

    pl.semaphore_wait(barrier, groups - 1 + 2)

    def h_copy(side):
        return pltpu.make_async_remote_copy(
            value_h.at[0 if side == 0 else heads - 1], hhalo.at[1 - side],
            h_send.at[side], h_recv.at[1 - side],
            device_id=(me, h_prev if side == 0 else h_next), device_id_type=MESH,
        )

    def x_copy(side):
        return pltpu.make_async_remote_copy(
            value_h.at[:, 0 if side == 0 else cells - 1], xhalo.at[1 - side],
            x_send.at[side], x_recv.at[1 - side],
            device_id=(me - 1 if side == 0 else me + 1, hb), device_id_type=MESH,
        )

    def pay_copy(d):
        peer = lax.rem(me + d, groups)
        return pltpu.make_async_remote_copy(
            pay.at[peer], got.at[d], pay_send.at[d], pay_recv.at[d],
            device_id=(peer, hb), device_id_type=MESH,
        )

    for side in range(2):
        h_copy(side).start()
    for side, has in ((0, has_prev), (1, has_next)):
        @pl.when(has)
        def _():
            x_copy(side).start()

    if groups <= 8:
        for d in range(groups - 1, 0, -1):
            pay_copy(d).start()
    else:
        pl.loop(1, groups)(lambda d: pay_copy(d).start())
    mine = pltpu.make_async_copy(pay.at[me], got.at[0], self_sem)
    mine.start()
    loads[6].wait()
    loads[7].wait()

    for side, has in ((0, has_prev), (1, has_next)):
        @pl.when(jnp.logical_not(has))
        def _():
            xhalo[side] = value[:, 0 if side == 0 else cells - 1]

    total = heads * blocks
    angles = [np.float32(2.0 * math.pi / total) * np.float32(k) for k in range(total)]
    cosines = [float(np.cos(a)) for a in angles]
    sines = [float(np.sin(a)) for a in angles]
    speed = SLOWEST + SPEED_RANGE * lax.broadcasted_iota(jnp.int32, (1, speeds), 1).astype(
        jnp.float32
    ) / (speeds - 1)
    cx = [pick(cosines, hb * heads + h) * speed for h in range(heads)]
    cy = [pick(sines, hb * heads + h) * speed for h in range(heads)]
    grid = [(h, x) for h in range(heads) for x in range(cells)]
    v = {(h, x): value[h, x] for h, x in grid}
    part, s_slope = {}, {}
    for h, x in grid:
        here = v[h, x]
        up, down = upper(here, 0), lower(here, 0)
        term = cy[h] * (up - down) * 0.5 - (up - 2.0 * here + down) * 0.5
        up, down = upper(here, 1), lower(here, 1)
        slope = 0.5 * (up - down)
        size = smooth_abs(slope)
        s_slope[h, x] = slope / size
        part[h, x] = term + ACCELERATION * size - ACCELERATION * 0.5 * (up - 2.0 * here + down)

    for side in range(2):
        h_copy(side).wait_recv()
    for side, has in ((0, has_prev), (1, has_next)):
        @pl.when(has)
        def _():
            x_copy(1 - side).wait_recv()
    for x in range(cells):
        v[-1, x] = hhalo[0, x]
        v[heads, x] = hhalo[1, x]
    for h in range(heads):
        v[h, -1] = xhalo[0, h]
        v[h, cells] = xhalo[1, h]

    share, h_slope = {}, {}
    for h, x in grid:
        here = v[h, x]
        up, down = v[h + 1, x], v[h - 1, x]
        slope = 0.5 * (up - down)
        size = smooth_abs(slope)
        h_slope[h, x] = slope / size
        turning = TURN_RATE * size - TURN_RATE * 0.5 * (up - 2.0 * here + down)
        up, down = v[h, x + 1], v[h, x - 1]
        across = cx[h] * (up - down) * 0.5 - (up - 2.0 * here + down) * 0.5
        relaxed = here - TIME_STEP * (across + part[h, x] + turning)
        floor = avoid[h, x]
        excess = SHARPNESS * (relaxed - floor)
        small = jnp.exp(-jnp.abs(excess))
        next_o[h, x] = floor + (jnp.maximum(excess, 0.0) + jnp.log1p(small)) / SHARPNESS
        inverse = 1.0 / (1.0 + small)
        positive = excess >= 0.0
        share[h, x] = (
            jnp.where(positive, 1.0, small) * inverse, jnp.where(positive, small, 1.0) * inverse
        )

    rows = heads * cells * lines
    row_id = lax.broadcasted_iota(jnp.int32, (rows, slots), 0).astype(jnp.float32)
    speed_id = lax.broadcasted_iota(jnp.int32, (speeds, slots), 0).astype(jnp.float32)

    def operands(d):
        one = got[d]
        cell = jnp.broadcast_to(one[4:5], (rows, slots))
        left = jnp.where(row_id == cell, one[0:1], jnp.where(row_id == cell + 1.0, one[1:2], 0.0))
        cell = jnp.broadcast_to(one[5:6], (speeds, slots))
        right = jnp.where(
            speed_id == cell, one[2:3], jnp.where(speed_id == cell + 1.0, one[3:4], 0.0)
        )
        return left, right

    def product(left, right):
        return lax.dot_general(
            left, right, (((1,), (1,)), ((), ())),
            precision=lax.Precision.HIGHEST, preferred_element_type=jnp.float32,
        )

    mine.wait()
    if groups <= 8:
        for d in range(1, groups):
            pay_copy(d).wait_recv()
        both = [operands(d) for d in range(groups)]
        deposit = product(
            jnp.concatenate([b[0] for b in both], 1), jnp.concatenate([b[1] for b in both], 1)
        )
    else:
        pl.loop(1, groups)(lambda d: pay_copy(d).wait_recv())
        deposit = lax.fori_loop(
            0, groups, lambda d, so_far: so_far + product(*operands(d)),
            jnp.zeros((rows, speeds), jnp.float32),
        )

    c = {}
    for n, (h, x) in enumerate(grid):
        adjoint = deposit[n * lines : (n + 1) * lines]
        c[h, x] = adjoint * share[h, x][0]
        carried[h, x] = c[h, x]
        agrad_o[h, x] = adjoint * share[h, x][1]
    ahead, back = {}, {}
    for h, x in grid:
        pull = (0.5 * TURN_RATE) * c[h, x] * h_slope[h, x]
        keep = (0.5 * TURN_RATE) * c[h, x]
        ahead[h, x] = pull - keep
        back[h, x] = -pull - keep
    for x in range(cells):
        turned[0, x] = back[0, x]
        turned[1, x] = ahead[heads - 1, x]

    def ch_copy(side):
        return pltpu.make_async_remote_copy(
            turned.at[side], chhalo.at[1 - side], ch_send.at[side], ch_recv.at[1 - side],
            device_id=(me, h_prev if side == 0 else h_next), device_id_type=MESH,
        )

    def cx_copy(side):
        return pltpu.make_async_remote_copy(
            carried.at[:, 0 if side == 0 else cells - 1], cxhalo.at[1 - side],
            cx_send.at[side], cx_recv.at[1 - side],
            device_id=(me - 1 if side == 0 else me + 1, hb), device_id_type=MESH,
        )

    for side, has in ((0, has_prev), (1, has_next)):
        @pl.when(has)
        def _():
            cx_copy(side).start()

        @pl.when(jnp.logical_not(has))
        def _():
            cxhalo[side] = jnp.zeros_like(cxhalo[side])
    for side in range(2):
        ch_copy(side).start()

    local = {}
    for h, x in grid:
        here = c[h, x]
        grad = spread((0.5 * cy[h] - 0.5) * here, (-0.5 * cy[h] - 0.5) * here, 0)
        pull = (0.5 * ACCELERATION) * here * s_slope[h, x]
        keep = (0.5 * ACCELERATION) * here
        grad = grad + spread(pull - keep, -pull - keep, 1)
        local[h, x] = grad + (2.0 + TURN_RATE + ACCELERATION) * here

    for side in range(2):
        ch_copy(side).wait_recv()
    for side, has in ((0, has_prev), (1, has_next)):
        @pl.when(has)
        def _():
            cx_copy(1 - side).wait_recv()
    for h, x in grid:
        grad = local[h, x]
        grad = grad + (ahead[h - 1, x] if h > 0 else chhalo[0, x])
        grad = grad + (back[h + 1, x] if h < heads - 1 else chhalo[1, x])
        low, high = 0.5 * cx[h] - 0.5, -0.5 * cx[h] - 0.5
        if x > 0:
            grad = grad + low * c[h, x - 1]
        else:
            grad = grad + jnp.where(has_prev, low * cxhalo[0, h], high * c[h, x])
        if x < cells - 1:
            grad = grad + high * c[h, x + 1]
        else:
            grad = grad + jnp.where(has_next, high * cxhalo[1, h], low * c[h, x])
        vgrad_o[h, x] = c[h, x] - TIME_STEP * grad

    for side in range(2):
        h_copy(side).wait_send()
        ch_copy(side).wait_send()
    for side, has in ((0, has_prev), (1, has_next)):
        @pl.when(has)
        def _():
            x_copy(side).wait_send()
            cx_copy(side).wait_send()
    if groups <= 8:
        for d in range(1, groups):
            pay_copy(d).wait_send()
    else:
        pl.loop(1, groups)(lambda d: pay_copy(d).wait_send())


def on_device(groups, blocks, value, avoid, weight, offy, offs, xy, hs, count):
    slots = weight.shape[3]
    value = jnp.transpose(value, (0, 2, 3, 1))
    avoid = jnp.transpose(avoid, (0, 2, 3, 1))
    weight, offy, offs, xy, hs = (a.reshape(groups, slots) for a in (weight, offy, offs, xy, hs))
    count = count.reshape(1, groups)
    heads, cells, lines, speeds = value.shape
    f32 = jnp.float32
    dma = pltpu.SemaphoreType.DMA
    field = pltpu.VMEM(value.shape, f32)
    x_pair = pltpu.VMEM((2, heads, lines, speeds), f32)
    h_pair = pltpu.VMEM((2, cells, lines, speeds), f32)
    outs = pl.pallas_call(
        functools.partial(kernel, groups, blocks),
        out_shape=[jax.ShapeDtypeStruct(value.shape, f32)] * 3,
        in_specs=[pl.BlockSpec(memory_space=pl.ANY)] * 8,
        out_specs=[pl.BlockSpec(memory_space=pltpu.VMEM)] * 3,
        scratch_shapes=[
            field, field,
            *[pltpu.VMEM((groups, slots), f32)] * 3,
            *[pltpu.VMEM((groups, slots), jnp.int32)] * 2,
            pltpu.VMEM((1, groups), jnp.int32),
            pltpu.VMEM((groups, ROWS, slots), f32), pltpu.VMEM((groups, ROWS, slots), f32),
            x_pair, h_pair, field, h_pair, x_pair, h_pair,
            dma((8,)), dma((groups,)), dma((groups,)),
            dma((2,)), dma((2,)), dma((2,)), dma((2,)),
            dma((2,)), dma((2,)), dma((2,)), dma((2,)), dma,
        ],
        compiler_params=pltpu.CompilerParams(collective_id=0, has_side_effects=True),
        name="step",
    )(value, avoid, weight, offy, offs, xy, hs, count)
    return tuple(jnp.transpose(o, (0, 3, 1, 2)) for o in outs)


def solution(mesh):
    field = P("ha", None, "gx", None)
    sample = P("gx", "ha", None, None)
    return jax.shard_map(
        functools.partial(on_device, mesh.shape["gx"], mesh.shape["ha"]),
        mesh=mesh,
        in_specs=(field, field, sample, sample, sample, sample, sample, P("gx", "ha", None)),
        out_specs=(field, field, field),
        check_vma=False,
    )
```

```python
import functools
import math

import jax
import jax.numpy as jnp
import numpy as np
from jax import lax
from jax.experimental import pallas as pl
from jax.experimental.pallas import tpu as pltpu
from jax.sharding import PartitionSpec as P

TIME_STEP = 0.3
SHARPNESS = 2.0
SOFTENING = 0.1
TURN_RATE = 0.5
ACCELERATION = 0.3
SLOWEST = 0.2
SPEED_RANGE = 0.8
ROWS = 8
MESH = pl.DeviceIdType.MESH


def smooth_abs(slope):
    return jnp.sqrt(slope * slope + SOFTENING * SOFTENING)


def upper(plane, axis):
    n = plane.shape[axis]
    return jnp.concatenate(
        [lax.slice_in_dim(plane, 1, n, axis=axis), lax.slice_in_dim(plane, n - 1, n, axis=axis)], axis
    )


def lower(plane, axis):
    n = plane.shape[axis]
    return jnp.concatenate(
        [lax.slice_in_dim(plane, 0, 1, axis=axis), lax.slice_in_dim(plane, 0, n - 1, axis=axis)], axis
    )


def spread(up, down, axis):
    n = up.shape[axis]
    from_lower = jnp.concatenate(
        [lax.slice_in_dim(down, 0, 1, axis=axis), lax.slice_in_dim(up, 0, n - 1, axis=axis)], axis
    )
    from_upper = jnp.concatenate(
        [lax.slice_in_dim(down, 1, n, axis=axis), lax.slice_in_dim(up, n - 1, n, axis=axis)], axis
    )
    return from_lower + from_upper


def pick(table, index):
    chosen = jnp.float32(table[0])
    for i in range(1, len(table)):
        chosen = jnp.where(index == i, jnp.float32(table[i]), chosen)
    return chosen


def kernel(
    groups, blocks,
    value_h, avoid_h, weight_h, offy_h, offs_h, xy_h, hs_h, count_h,
    next_o, vgrad_o, agrad_o,
    value, avoid, weight, offy, offs, xy, hs, count,
    pay, got, xhalo, hhalo, carried, turned, cxhalo, chhalo,
    in_sem, pay_send, pay_recv, x_send, x_recv, h_send, h_recv,
    cx_send, cx_recv, ch_send, ch_recv, self_sem,
):
    heads, cells, lines, speeds = value.shape
    slots = weight.shape[1]
    me = lax.axis_index("gx")
    hb = lax.axis_index("ha")
    h_next = lax.rem(hb + 1, blocks)
    h_prev = lax.rem(hb + blocks - 1, blocks)
    has_prev = me > 0
    has_next = me < groups - 1

    barrier = pltpu.get_barrier_semaphore()

    def greet(d):
        pl.semaphore_signal(
            barrier, inc=1, device_id=(lax.rem(me + d, groups), hb), device_id_type=MESH
        )

    if groups <= 8:
        for d in range(1, groups):
            greet(d)
    else:
        pl.loop(1, groups)(greet)
    for other in (h_prev, h_next):
        pl.semaphore_signal(barrier, inc=1, device_id=(me, other), device_id_type=MESH)

    pairs = (
        (weight_h, weight), (offy_h, offy), (offs_h, offs), (xy_h, xy), (hs_h, hs), (count_h, count),
        (value_h, value), (avoid_h, avoid),
    )
    loads = [pltpu.make_async_copy(a, b, in_sem.at[i]) for i, (a, b) in enumerate(pairs)]
    for load in loads:
        load.start()
    for load in loads[:6]:
        load.wait()

    owners = lax.broadcasted_iota(jnp.int32, (groups, groups), 0)
    lanes = lax.broadcasted_iota(jnp.int32, (groups, groups), 1)
    live = jnp.sum(
        jnp.where(owners == lanes, jnp.broadcast_to(count[...], (groups, groups)), 0).astype(jnp.float32),
        axis=1, keepdims=True,
    )
    slot = lax.broadcasted_iota(jnp.int32, (groups, slots), 1).astype(jnp.float32)
    w = jnp.where(slot < live, weight[...], 0.0)
    oy = offy[...]
    os = offs[...]
    state = hs[...]
    head = lax.div(state, speeds)
    pay[:, 0, :] = w * (1.0 - oy)
    pay[:, 1, :] = w * oy
    pay[:, 2, :] = 1.0 - os
    pay[:, 3, :] = os
    pay[:, 4, :] = (head * (cells * lines) + xy[...]).astype(jnp.float32)
    pay[:, 5, :] = (state - head * speeds).astype(jnp.float32)
    pay[:, 6, :] = jnp.zeros((groups, slots), jnp.float32)
    pay[:, 7, :] = jnp.zeros((groups, slots), jnp.float32)

    pl.semaphore_wait(barrier, groups - 1 + 2)

    def h_copy(side):
        return pltpu.make_async_remote_copy(
            value_h.at[0 if side == 0 else heads - 1], hhalo.at[1 - side],
            h_send.at[side], h_recv.at[1 - side],
            device_id=(me, h_prev if side == 0 else h_next), device_id_type=MESH,
        )

    def x_copy(side):
        return pltpu.make_async_remote_copy(
            value_h.at[:, 0 if side == 0 else cells - 1], xhalo.at[1 - side],
            x_send.at[side], x_recv.at[1 - side],
            device_id=(me - 1 if side == 0 else me + 1, hb), device_id_type=MESH,
        )

    def pay_copy(d):
        peer = lax.rem(me + d, groups)
        return pltpu.make_async_remote_copy(
            pay.at[peer], got.at[d], pay_send.at[d], pay_recv.at[d],
            device_id=(peer, hb), device_id_type=MESH,
        )

    for side in range(2):
        h_copy(side).start()
    for side, has in ((0, has_prev), (1, has_next)):
        @pl.when(has)
        def _():
            x_copy(side).start()

    if groups <= 8:
        for d in range(groups - 1, 0, -1):
            pay_copy(d).start()
    else:
        pl.loop(1, groups)(lambda d: pay_copy(d).start())
    mine = pltpu.make_async_copy(pay.at[me], got.at[0], self_sem)
    mine.start()
    loads[6].wait()
    loads[7].wait()

    for side, has in ((0, has_prev), (1, has_next)):
        @pl.when(jnp.logical_not(has))
        def _():
            xhalo[side] = value[:, 0 if side == 0 else cells - 1]

    total = heads * blocks
    angles = [np.float32(2.0 * math.pi / total) * np.float32(k) for k in range(total)]
    cosines = [float(np.cos(a)) for a in angles]
    sines = [float(np.sin(a)) for a in angles]
    speed = SLOWEST + SPEED_RANGE * lax.broadcasted_iota(jnp.int32, (1, speeds), 1).astype(
        jnp.float32
    ) / (speeds - 1)
    cx = [pick(cosines, hb * heads + h) * speed for h in range(heads)]
    cy = [pick(sines, hb * heads + h) * speed for h in range(heads)]
    grid = [(h, x) for h in range(heads) for x in range(cells)]
    v = {(h, x): value[h, x] for h, x in grid}
    part, s_slope = {}, {}
    for h, x in grid:
        here = v[h, x]
        up, down = upper(here, 0), lower(here, 0)
        term = cy[h] * (up - down) * 0.5 - (up - 2.0 * here + down) * 0.5
        up, down = upper(here, 1), lower(here, 1)
        slope = 0.5 * (up - down)
        size = smooth_abs(slope)
        s_slope[h, x] = slope / size
        part[h, x] = term + ACCELERATION * size - ACCELERATION * 0.5 * (up - 2.0 * here + down)

    for side in range(2):
        h_copy(side).wait_recv()
    for side, has in ((0, has_prev), (1, has_next)):
        @pl.when(has)
        def _():
            x_copy(1 - side).wait_recv()
    for x in range(cells):
        v[-1, x] = hhalo[0, x]
        v[heads, x] = hhalo[1, x]
    for h in range(heads):
        v[h, -1] = xhalo[0, h]
        v[h, cells] = xhalo[1, h]

    share, h_slope = {}, {}
    for h, x in grid:
        here = v[h, x]
        up, down = v[h + 1, x], v[h - 1, x]
        slope = 0.5 * (up - down)
        size = smooth_abs(slope)
        h_slope[h, x] = slope / size
        turning = TURN_RATE * size - TURN_RATE * 0.5 * (up - 2.0 * here + down)
        up, down = v[h, x + 1], v[h, x - 1]
        across = cx[h] * (up - down) * 0.5 - (up - 2.0 * here + down) * 0.5
        relaxed = here - TIME_STEP * (across + part[h, x] + turning)
        floor = avoid[h, x]
        excess = SHARPNESS * (relaxed - floor)
        small = jnp.exp(-jnp.abs(excess))
        next_o[h, x] = floor + (jnp.maximum(excess, 0.0) + jnp.log1p(small)) / SHARPNESS
        inverse = 1.0 / (1.0 + small)
        positive = excess >= 0.0
        share[h, x] = (
            jnp.where(positive, 1.0, small) * inverse, jnp.where(positive, small, 1.0) * inverse
        )

    rows = heads * cells * lines
    row_id = lax.broadcasted_iota(jnp.int32, (rows, slots), 0).astype(jnp.float32)
    speed_id = lax.broadcasted_iota(jnp.int32, (speeds, slots), 0).astype(jnp.float32)

    def operands(d):
        one = got[d]
        cell = jnp.broadcast_to(one[4:5], (rows, slots))
        left = jnp.where(row_id == cell, one[0:1], jnp.where(row_id == cell + 1.0, one[1:2], 0.0))
        cell = jnp.broadcast_to(one[5:6], (speeds, slots))
        right = jnp.where(
            speed_id == cell, one[2:3], jnp.where(speed_id == cell + 1.0, one[3:4], 0.0)
        )
        return left, right

    def product(left, right):
        return lax.dot_general(
            left, right, (((1,), (1,)), ((), ())),
            precision=lax.Precision.HIGHEST, preferred_element_type=jnp.float32,
        )

    mine.wait()
    if groups <= 8:
        for d in range(1, groups):
            pay_copy(d).wait_recv()
        both = [operands(d) for d in range(groups)]
        deposit = product(
            jnp.concatenate([b[0] for b in both], 1), jnp.concatenate([b[1] for b in both], 1)
        )
    else:
        pl.loop(1, groups)(lambda d: pay_copy(d).wait_recv())
        deposit = lax.fori_loop(
            0, groups, lambda d, so_far: so_far + product(*operands(d)),
            jnp.zeros((rows, speeds), jnp.float32),
        )

    c = {}
    for n, (h, x) in enumerate(grid):
        adjoint = deposit[n * lines : (n + 1) * lines]
        c[h, x] = adjoint * share[h, x][0]
        carried[h, x] = c[h, x]
        agrad_o[h, x] = adjoint * share[h, x][1]
    ahead, back = {}, {}
    for h, x in grid:
        pull = (0.5 * TURN_RATE) * c[h, x] * h_slope[h, x]
        keep = (0.5 * TURN_RATE) * c[h, x]
        ahead[h, x] = pull - keep
        back[h, x] = -pull - keep
    for x in range(cells):
        turned[0, x] = back[0, x]
        turned[1, x] = ahead[heads - 1, x]

    def ch_copy(side):
        return pltpu.make_async_remote_copy(
            turned.at[side], chhalo.at[1 - side], ch_send.at[side], ch_recv.at[1 - side],
            device_id=(me, h_prev if side == 0 else h_next), device_id_type=MESH,
        )

    def cx_copy(side):
        return pltpu.make_async_remote_copy(
            carried.at[:, 0 if side == 0 else cells - 1], cxhalo.at[1 - side],
            cx_send.at[side], cx_recv.at[1 - side],
            device_id=(me - 1 if side == 0 else me + 1, hb), device_id_type=MESH,
        )

    for side, has in ((0, has_prev), (1, has_next)):
        @pl.when(has)
        def _():
            cx_copy(side).start()

        @pl.when(jnp.logical_not(has))
        def _():
            cxhalo[side] = jnp.zeros_like(cxhalo[side])
    for side in range(2):
        ch_copy(side).start()

    local = {}
    for h, x in grid:
        here = c[h, x]
        grad = spread((0.5 * cy[h] - 0.5) * here, (-0.5 * cy[h] - 0.5) * here, 0)
        pull = (0.5 * ACCELERATION) * here * s_slope[h, x]
        keep = (0.5 * ACCELERATION) * here
        grad = grad + spread(pull - keep, -pull - keep, 1)
        local[h, x] = grad + (2.0 + TURN_RATE + ACCELERATION) * here

    for side in range(2):
        ch_copy(side).wait_recv()
    for side, has in ((0, has_prev), (1, has_next)):
        @pl.when(has)
        def _():
            cx_copy(1 - side).wait_recv()
    for h, x in grid:
        grad = local[h, x]
        grad = grad + (ahead[h - 1, x] if h > 0 else chhalo[0, x])
        grad = grad + (back[h + 1, x] if h < heads - 1 else chhalo[1, x])
        low, high = 0.5 * cx[h] - 0.5, -0.5 * cx[h] - 0.5
        if x > 0:
            grad = grad + low * c[h, x - 1]
        else:
            grad = grad + jnp.where(has_prev, low * cxhalo[0, h], high * c[h, x])
        if x < cells - 1:
            grad = grad + high * c[h, x + 1]
        else:
            grad = grad + jnp.where(has_next, high * cxhalo[1, h], low * c[h, x])
        vgrad_o[h, x] = c[h, x] - TIME_STEP * grad

    for side in range(2):
        h_copy(side).wait_send()
        ch_copy(side).wait_send()
    for side, has in ((0, has_prev), (1, has_next)):
        @pl.when(has)
        def _():
            x_copy(side).wait_send()
            cx_copy(side).wait_send()
    if groups <= 8:
        for d in range(1, groups):
            pay_copy(d).wait_send()
    else:
        pl.loop(1, groups)(lambda d: pay_copy(d).wait_send())


def write_out(next_v, vgrad_v, agrad_v, next_o, vgrad_o, agrad_o, sem):
    copies = [
        pltpu.make_async_copy(a, b, sem.at[i])
        for i, (a, b) in enumerate(((next_v, next_o), (vgrad_v, vgrad_o), (agrad_v, agrad_o)))
    ]
    for copy in copies:
        copy.start()
    for copy in copies:
        copy.wait()


def on_device(groups, blocks, value, avoid, weight, offy, offs, xy, hs, count):
    slots = weight.shape[3]
    value = jnp.transpose(value, (0, 2, 3, 1))
    avoid = jnp.transpose(avoid, (0, 2, 3, 1))
    weight, offy, offs, xy, hs = (a.reshape(groups, slots) for a in (weight, offy, offs, xy, hs))
    count = count.reshape(1, groups)
    heads, cells, lines, speeds = value.shape
    f32 = jnp.float32
    dma = pltpu.SemaphoreType.DMA
    field = pltpu.VMEM(value.shape, f32)
    x_pair = pltpu.VMEM((2, heads, lines, speeds), f32)
    h_pair = pltpu.VMEM((2, cells, lines, speeds), f32)
    outs = pl.pallas_call(
        functools.partial(kernel, groups, blocks),
        out_shape=[pltpu.VMEM(value.shape, f32)] * 3,
        in_specs=[pl.BlockSpec(memory_space=pltpu.HBM)] * 8,
        out_specs=[pl.BlockSpec(memory_space=pltpu.VMEM)] * 3,
        scratch_shapes=[
            field, field,
            *[pltpu.VMEM((groups, slots), f32)] * 3,
            *[pltpu.VMEM((groups, slots), jnp.int32)] * 2,
            pltpu.VMEM((1, groups), jnp.int32),
            pltpu.VMEM((groups, ROWS, slots), f32), pltpu.VMEM((groups, ROWS, slots), f32),
            x_pair, h_pair, field, h_pair, x_pair, h_pair,
            dma((8,)), dma((groups,)), dma((groups,)),
            dma((2,)), dma((2,)), dma((2,)), dma((2,)),
            dma((2,)), dma((2,)), dma((2,)), dma((2,)), dma,
        ],
        compiler_params=pltpu.CompilerParams(collective_id=0, has_side_effects=True),
        name="step",
    )(value, avoid, weight, offy, offs, xy, hs, count)
    outs = pl.pallas_call(
        write_out,
        out_shape=[jax.ShapeDtypeStruct(value.shape, f32)] * 3,
        in_specs=[pl.BlockSpec(memory_space=pl.ANY)] * 3,
        out_specs=[pl.BlockSpec(memory_space=pl.ANY)] * 3,
        scratch_shapes=[dma((3,))],
        compiler_params=pltpu.CompilerParams(vmem_limit_bytes=1 << 20),
        name="write_out",
    )(*outs)
    return tuple(jnp.transpose(o, (0, 3, 1, 2)) for o in outs)


def solution(mesh):
    field = P("ha", None, "gx", None)
    sample = P("gx", "ha", None, None)
    return jax.shard_map(
        functools.partial(on_device, mesh.shape["gx"], mesh.shape["ha"]),
        mesh=mesh,
        in_specs=(field, field, sample, sample, sample, sample, sample, P("gx", "ha", None)),
        out_specs=(field, field, field),
        check_vma=False,
    )
```

```python
import functools
import math

import jax
import jax.numpy as jnp
import numpy as np
from jax import lax
from jax.experimental import pallas as pl
from jax.experimental.pallas import tpu as pltpu
from jax.sharding import PartitionSpec as P

TIME_STEP = 0.3
SHARPNESS = 2.0
SOFTENING = 0.1
TURN_RATE = 0.5
ACCELERATION = 0.3
SLOWEST = 0.2
SPEED_RANGE = 0.8
ROWS = 8
MESH = pl.DeviceIdType.MESH


def smooth_abs(slope):
    return jnp.sqrt(slope * slope + SOFTENING * SOFTENING)


def upper(plane, axis):
    n = plane.shape[axis]
    return jnp.concatenate(
        [lax.slice_in_dim(plane, 1, n, axis=axis), lax.slice_in_dim(plane, n - 1, n, axis=axis)], axis
    )


def lower(plane, axis):
    n = plane.shape[axis]
    return jnp.concatenate(
        [lax.slice_in_dim(plane, 0, 1, axis=axis), lax.slice_in_dim(plane, 0, n - 1, axis=axis)], axis
    )


def spread(up, down, axis):
    n = up.shape[axis]
    from_lower = jnp.concatenate(
        [lax.slice_in_dim(down, 0, 1, axis=axis), lax.slice_in_dim(up, 0, n - 1, axis=axis)], axis
    )
    from_upper = jnp.concatenate(
        [lax.slice_in_dim(down, 1, n, axis=axis), lax.slice_in_dim(up, n - 1, n, axis=axis)], axis
    )
    return from_lower + from_upper


def pick(table, index):
    chosen = jnp.float32(table[0])
    for i in range(1, len(table)):
        chosen = jnp.where(index == i, jnp.float32(table[i]), chosen)
    return chosen


def kernel(
    groups, blocks,
    value_h, avoid_h, weight_h, offy_h, offs_h, xy_h, hs_h, count_h,
    next_o, vgrad_o, agrad_o,
    value, avoid, weight, offy, offs, xy, hs, count,
    pay, got, xhalo, hhalo, carried, turned, cxhalo, chhalo,
    in_sem, pay_send, pay_recv, x_send, x_recv, h_send, h_recv,
    cx_send, cx_recv, ch_send, ch_recv, self_sem,
):
    heads, cells, lines, speeds = value.shape
    slots = weight.shape[1]
    me = lax.axis_index("gx")
    hb = lax.axis_index("ha")
    h_next = lax.rem(hb + 1, blocks)
    h_prev = lax.rem(hb + blocks - 1, blocks)
    has_prev = me > 0
    has_next = me < groups - 1

    barrier = pltpu.get_barrier_semaphore()

    def greet(d):
        pl.semaphore_signal(
            barrier, inc=1, device_id=(lax.rem(me + d, groups), hb), device_id_type=MESH
        )

    if groups <= 8:
        for d in range(1, groups):
            greet(d)
    else:
        pl.loop(1, groups)(greet)
    for other in (h_prev, h_next):
        pl.semaphore_signal(barrier, inc=1, device_id=(me, other), device_id_type=MESH)

    pairs = (
        (weight_h, weight), (offy_h, offy), (offs_h, offs), (xy_h, xy), (hs_h, hs), (count_h, count),
        (value_h, value), (avoid_h, avoid),
    )
    loads = [pltpu.make_async_copy(a, b, in_sem.at[i]) for i, (a, b) in enumerate(pairs)]
    for load in loads:
        load.start()
    for load in loads[:6]:
        load.wait()

    owners = lax.broadcasted_iota(jnp.int32, (groups, groups), 0)
    lanes = lax.broadcasted_iota(jnp.int32, (groups, groups), 1)
    live = jnp.sum(
        jnp.where(owners == lanes, jnp.broadcast_to(count[...], (groups, groups)), 0).astype(jnp.float32),
        axis=1, keepdims=True,
    )
    slot = lax.broadcasted_iota(jnp.int32, (groups, slots), 1).astype(jnp.float32)
    w = jnp.where(slot < live, weight[...], 0.0)
    oy = offy[...]
    os = offs[...]
    state = hs[...]
    head = lax.div(state, speeds)
    pay[:, 0, :] = w * (1.0 - oy)
    pay[:, 1, :] = w * oy
    pay[:, 2, :] = 1.0 - os
    pay[:, 3, :] = os
    pay[:, 4, :] = (head * (cells * lines) + xy[...]).astype(jnp.float32)
    pay[:, 5, :] = (state - head * speeds).astype(jnp.float32)
    pay[:, 6, :] = jnp.zeros((groups, slots), jnp.float32)
    pay[:, 7, :] = jnp.zeros((groups, slots), jnp.float32)

    loads[6].wait()
    pl.semaphore_wait(barrier, groups - 1 + 2)

    def h_copy(side):
        return pltpu.make_async_remote_copy(
            value.at[0 if side == 0 else heads - 1], hhalo.at[1 - side],
            h_send.at[side], h_recv.at[1 - side],
            device_id=(me, h_prev if side == 0 else h_next), device_id_type=MESH,
        )

    def x_copy(side):
        return pltpu.make_async_remote_copy(
            value.at[:, 0 if side == 0 else cells - 1], xhalo.at[1 - side],
            x_send.at[side], x_recv.at[1 - side],
            device_id=(me - 1 if side == 0 else me + 1, hb), device_id_type=MESH,
        )

    def pay_copy(d):
        peer = lax.rem(me + d, groups)
        return pltpu.make_async_remote_copy(
            pay.at[peer], got.at[d], pay_send.at[d], pay_recv.at[d],
            device_id=(peer, hb), device_id_type=MESH,
        )

    for side in range(2):
        h_copy(side).start()
    for side, has in ((0, has_prev), (1, has_next)):
        @pl.when(has)
        def _():
            x_copy(side).start()

    if groups <= 8:
        for d in range(groups - 1, 0, -1):
            pay_copy(d).start()
    else:
        pl.loop(1, groups)(lambda d: pay_copy(d).start())
    mine = pltpu.make_async_copy(pay.at[me], got.at[0], self_sem)
    mine.start()
    loads[7].wait()

    for side, has in ((0, has_prev), (1, has_next)):
        @pl.when(jnp.logical_not(has))
        def _():
            xhalo[side] = value[:, 0 if side == 0 else cells - 1]

    total = heads * blocks
    angles = [np.float32(2.0 * math.pi / total) * np.float32(k) for k in range(total)]
    cosines = [float(np.cos(a)) for a in angles]
    sines = [float(np.sin(a)) for a in angles]
    speed = SLOWEST + SPEED_RANGE * lax.broadcasted_iota(jnp.int32, (1, speeds), 1).astype(
        jnp.float32
    ) / (speeds - 1)
    cx = [pick(cosines, hb * heads + h) * speed for h in range(heads)]
    cy = [pick(sines, hb * heads + h) * speed for h in range(heads)]
    grid = [(h, x) for h in range(heads) for x in range(cells)]
    v = {(h, x): value[h, x] for h, x in grid}
    part, s_slope = {}, {}
    for h, x in grid:
        here = v[h, x]
        up, down = upper(here, 0), lower(here, 0)
        term = cy[h] * (up - down) * 0.5 - (up - 2.0 * here + down) * 0.5
        up, down = upper(here, 1), lower(here, 1)
        slope = 0.5 * (up - down)
        size = smooth_abs(slope)
        s_slope[h, x] = slope / size
        part[h, x] = term + ACCELERATION * size - ACCELERATION * 0.5 * (up - 2.0 * here + down)

    for side in range(2):
        h_copy(side).wait_recv()
    for side, has in ((0, has_prev), (1, has_next)):
        @pl.when(has)
        def _():
            x_copy(1 - side).wait_recv()
    for x in range(cells):
        v[-1, x] = hhalo[0, x]
        v[heads, x] = hhalo[1, x]
    for h in range(heads):
        v[h, -1] = xhalo[0, h]
        v[h, cells] = xhalo[1, h]

    share, h_slope, above = {}, {}, {}
    for h, x in grid:
        here = v[h, x]
        up, down = v[h + 1, x], v[h - 1, x]
        slope = 0.5 * (up - down)
        size = smooth_abs(slope)
        h_slope[h, x] = slope / size
        turning = TURN_RATE * size - TURN_RATE * 0.5 * (up - 2.0 * here + down)
        up, down = v[h, x + 1], v[h, x - 1]
        across = cx[h] * (up - down) * 0.5 - (up - 2.0 * here + down) * 0.5
        relaxed = here - TIME_STEP * (across + part[h, x] + turning)
        floor = avoid[h, x]
        excess = SHARPNESS * (relaxed - floor)
        small = jnp.exp(-jnp.abs(excess))
        share[h, x] = jnp.where(excess >= 0.0, 1.0, small) / (1.0 + small)
        above[h, x] = (excess, small)

    rows = heads * cells * lines
    row_id = lax.broadcasted_iota(jnp.int32, (rows, slots), 0).astype(jnp.float32)
    speed_id = lax.broadcasted_iota(jnp.int32, (speeds, slots), 0).astype(jnp.float32)

    def operands(d):
        one = got[d]
        cell = jnp.broadcast_to(one[4:5], (rows, slots))
        left = jnp.where(row_id == cell, one[0:1], jnp.where(row_id == cell + 1.0, one[1:2], 0.0))
        cell = jnp.broadcast_to(one[5:6], (speeds, slots))
        right = jnp.where(
            speed_id == cell, one[2:3], jnp.where(speed_id == cell + 1.0, one[3:4], 0.0)
        )
        return left, right

    def product(left, right):
        return lax.dot_general(
            left, right, (((1,), (1,)), ((), ())),
            precision=lax.Precision.HIGHEST, preferred_element_type=jnp.float32,
        )

    mine.wait()
    if groups <= 8:
        for d in range(1, groups):
            pay_copy(d).wait_recv()
        both = [operands(d) for d in range(groups)]
        deposit = product(
            jnp.concatenate([b[0] for b in both], 1), jnp.concatenate([b[1] for b in both], 1)
        )
    else:
        pl.loop(1, groups)(lambda d: pay_copy(d).wait_recv())
        deposit = lax.fori_loop(
            0, groups, lambda d, so_far: so_far + product(*operands(d)),
            jnp.zeros((rows, speeds), jnp.float32),
        )

    c, adj = {}, {}
    for n, (h, x) in enumerate(grid):
        adjoint = deposit[n * lines : (n + 1) * lines]
        c[h, x] = adjoint * share[h, x]
        carried[h, x] = c[h, x]
        adj[h, x] = adjoint
    ahead, back = {}, {}
    for h, x in grid:
        pull = (0.5 * TURN_RATE) * c[h, x] * h_slope[h, x]
        keep = (0.5 * TURN_RATE) * c[h, x]
        ahead[h, x] = pull - keep
        back[h, x] = -pull - keep
    for x in range(cells):
        turned[0, x] = back[0, x]
        turned[1, x] = ahead[heads - 1, x]

    def ch_copy(side):
        return pltpu.make_async_remote_copy(
            turned.at[side], chhalo.at[1 - side], ch_send.at[side], ch_recv.at[1 - side],
            device_id=(me, h_prev if side == 0 else h_next), device_id_type=MESH,
        )

    def cx_copy(side):
        return pltpu.make_async_remote_copy(
            carried.at[:, 0 if side == 0 else cells - 1], cxhalo.at[1 - side],
            cx_send.at[side], cx_recv.at[1 - side],
            device_id=(me - 1 if side == 0 else me + 1, hb), device_id_type=MESH,
        )

    for side, has in ((0, has_prev), (1, has_next)):
        @pl.when(has)
        def _():
            cx_copy(side).start()

        @pl.when(jnp.logical_not(has))
        def _():
            cxhalo[side] = jnp.zeros_like(cxhalo[side])
    for side in range(2):
        ch_copy(side).start()

    local = {}
    for h, x in grid:
        excess, small = above[h, x]
        next_o[h, x] = avoid[h, x] + (jnp.maximum(excess, 0.0) + jnp.log1p(small)) / SHARPNESS
        agrad_o[h, x] = adj[h, x] * (jnp.where(excess >= 0.0, small, 1.0) / (1.0 + small))
        here = c[h, x]
        grad = spread((0.5 * cy[h] - 0.5) * here, (-0.5 * cy[h] - 0.5) * here, 0)
        pull = (0.5 * ACCELERATION) * here * s_slope[h, x]
        keep = (0.5 * ACCELERATION) * here
        grad = grad + spread(pull - keep, -pull - keep, 1)
        local[h, x] = grad + (2.0 + TURN_RATE + ACCELERATION) * here

    for side in range(2):
        ch_copy(side).wait_recv()
    for side, has in ((0, has_prev), (1, has_next)):
        @pl.when(has)
        def _():
            cx_copy(1 - side).wait_recv()
    for h, x in grid:
        grad = local[h, x]
        grad = grad + (ahead[h - 1, x] if h > 0 else chhalo[0, x])
        grad = grad + (back[h + 1, x] if h < heads - 1 else chhalo[1, x])
        low, high = 0.5 * cx[h] - 0.5, -0.5 * cx[h] - 0.5
        if x > 0:
            grad = grad + low * c[h, x - 1]
        else:
            grad = grad + jnp.where(has_prev, low * cxhalo[0, h], high * c[h, x])
        if x < cells - 1:
            grad = grad + high * c[h, x + 1]
        else:
            grad = grad + jnp.where(has_next, high * cxhalo[1, h], low * c[h, x])
        vgrad_o[h, x] = c[h, x] - TIME_STEP * grad

    for side in range(2):
        h_copy(side).wait_send()
        ch_copy(side).wait_send()
    for side, has in ((0, has_prev), (1, has_next)):
        @pl.when(has)
        def _():
            x_copy(side).wait_send()
            cx_copy(side).wait_send()
    if groups <= 8:
        for d in range(1, groups):
            pay_copy(d).wait_send()
    else:
        pl.loop(1, groups)(lambda d: pay_copy(d).wait_send())


def write_out(next_v, vgrad_v, agrad_v, next_o, vgrad_o, agrad_o, sem):
    copies = [
        pltpu.make_async_copy(a, b, sem.at[i])
        for i, (a, b) in enumerate(((next_v, next_o), (vgrad_v, vgrad_o), (agrad_v, agrad_o)))
    ]
    for copy in copies:
        copy.start()
    for copy in copies:
        copy.wait()


def on_device(groups, blocks, value, avoid, weight, offy, offs, xy, hs, count):
    slots = weight.shape[3]
    value = jnp.transpose(value, (0, 2, 3, 1))
    avoid = jnp.transpose(avoid, (0, 2, 3, 1))
    weight, offy, offs, xy, hs = (a.reshape(groups, slots) for a in (weight, offy, offs, xy, hs))
    count = count.reshape(1, groups)
    heads, cells, lines, speeds = value.shape
    f32 = jnp.float32
    dma = pltpu.SemaphoreType.DMA
    field = pltpu.VMEM(value.shape, f32)
    x_pair = pltpu.VMEM((2, heads, lines, speeds), f32)
    h_pair = pltpu.VMEM((2, cells, lines, speeds), f32)
    outs = pl.pallas_call(
        functools.partial(kernel, groups, blocks),
        out_shape=[pltpu.VMEM(value.shape, f32)] * 3,
        in_specs=[pl.BlockSpec(memory_space=pltpu.HBM)] * 8,
        out_specs=[pl.BlockSpec(memory_space=pltpu.VMEM)] * 3,
        scratch_shapes=[
            field, field,
            *[pltpu.VMEM((groups, slots), f32)] * 3,
            *[pltpu.VMEM((groups, slots), jnp.int32)] * 2,
            pltpu.VMEM((1, groups), jnp.int32),
            pltpu.VMEM((groups, ROWS, slots), f32), pltpu.VMEM((groups, ROWS, slots), f32),
            x_pair, h_pair, field, h_pair, x_pair, h_pair,
            dma((8,)), dma((groups,)), dma((groups,)),
            dma((2,)), dma((2,)), dma((2,)), dma((2,)),
            dma((2,)), dma((2,)), dma((2,)), dma((2,)), dma,
        ],
        compiler_params=pltpu.CompilerParams(collective_id=0, has_side_effects=True),
        name="step",
    )(value, avoid, weight, offy, offs, xy, hs, count)
    outs = pl.pallas_call(
        write_out,
        out_shape=[jax.ShapeDtypeStruct(value.shape, f32)] * 3,
        in_specs=[pl.BlockSpec(memory_space=pl.ANY)] * 3,
        out_specs=[pl.BlockSpec(memory_space=pl.ANY)] * 3,
        scratch_shapes=[dma((3,))],
        compiler_params=pltpu.CompilerParams(vmem_limit_bytes=1 << 20),
        name="write_out",
    )(*outs)
    return tuple(jnp.transpose(o, (0, 3, 1, 2)) for o in outs)


def solution(mesh):
    field = P("ha", None, "gx", None)
    sample = P("gx", "ha", None, None)
    return jax.shard_map(
        functools.partial(on_device, mesh.shape["gx"], mesh.shape["ha"]),
        mesh=mesh,
        in_specs=(field, field, sample, sample, sample, sample, sample, P("gx", "ha", None)),
        out_specs=(field, field, field),
        check_vma=False,
    )
```

```python
import functools
import math

import jax
import jax.numpy as jnp
import numpy as np
from jax import lax
from jax.experimental import pallas as pl
from jax.experimental.pallas import tpu as pltpu
from jax.sharding import PartitionSpec as P

TIME_STEP = 0.3
SHARPNESS = 2.0
SOFTENING = 0.1
TURN_RATE = 0.5
ACCELERATION = 0.3
SLOWEST = 0.2
SPEED_RANGE = 0.8
ROWS = 8
MESH = pl.DeviceIdType.MESH


def smooth_abs(slope):
    return jnp.sqrt(slope * slope + SOFTENING * SOFTENING)


def upper(plane, axis):
    n = plane.shape[axis]
    return jnp.concatenate(
        [lax.slice_in_dim(plane, 1, n, axis=axis), lax.slice_in_dim(plane, n - 1, n, axis=axis)], axis
    )


def lower(plane, axis):
    n = plane.shape[axis]
    return jnp.concatenate(
        [lax.slice_in_dim(plane, 0, 1, axis=axis), lax.slice_in_dim(plane, 0, n - 1, axis=axis)], axis
    )


def spread(up, down, axis):
    n = up.shape[axis]
    from_lower = jnp.concatenate(
        [lax.slice_in_dim(down, 0, 1, axis=axis), lax.slice_in_dim(up, 0, n - 1, axis=axis)], axis
    )
    from_upper = jnp.concatenate(
        [lax.slice_in_dim(down, 1, n, axis=axis), lax.slice_in_dim(up, n - 1, n, axis=axis)], axis
    )
    return from_lower + from_upper


def pick(table, index):
    chosen = jnp.float32(table[0])
    for i in range(1, len(table)):
        chosen = jnp.where(index == i, jnp.float32(table[i]), chosen)
    return chosen


def kernel(
    groups, blocks,
    value_h, avoid_h, weight_h, offy_h, offs_h, xy_h, hs_h, count_h,
    next_o, vgrad_o, agrad_o,
    value, avoid, weight, offy, offs, xy, hs, count,
    pay, got, xhalo, hhalo, carried, turned, cxhalo, chhalo,
    in_sem, pay_send, pay_recv, x_send, x_recv, h_send, h_recv,
    cx_send, cx_recv, ch_send, ch_recv, self_sem,
):
    heads, cells, lines, speeds = value.shape
    slots = weight.shape[1]
    me = lax.axis_index("gx")
    hb = lax.axis_index("ha")
    h_next = lax.rem(hb + 1, blocks)
    h_prev = lax.rem(hb + blocks - 1, blocks)
    has_prev = me > 0
    has_next = me < groups - 1

    barrier = pltpu.get_barrier_semaphore()

    def greet(d):
        pl.semaphore_signal(
            barrier, inc=1, device_id=(lax.rem(me + d, groups), hb), device_id_type=MESH
        )

    if groups <= 8:
        for d in range(1, groups):
            greet(d)
    else:
        pl.loop(1, groups)(greet)
    for other in (h_prev, h_next):
        pl.semaphore_signal(barrier, inc=1, device_id=(me, other), device_id_type=MESH)

    pairs = (
        (weight_h, weight), (offy_h, offy), (offs_h, offs), (xy_h, xy), (hs_h, hs), (count_h, count),
        (value_h, value), (avoid_h, avoid),
    )
    loads = [pltpu.make_async_copy(a, b, in_sem.at[i]) for i, (a, b) in enumerate(pairs)]
    for load in loads:
        load.start()
    for load in loads[:6]:
        load.wait()

    owners = lax.broadcasted_iota(jnp.int32, (groups, groups), 0)
    lanes = lax.broadcasted_iota(jnp.int32, (groups, groups), 1)
    live = jnp.sum(
        jnp.where(owners == lanes, jnp.broadcast_to(count[...], (groups, groups)), 0).astype(jnp.float32),
        axis=1, keepdims=True,
    )
    slot = lax.broadcasted_iota(jnp.int32, (groups, slots), 1).astype(jnp.float32)
    w = jnp.where(slot < live, weight[...], 0.0)
    oy = offy[...]
    os = offs[...]
    state = hs[...]
    head = lax.div(state, speeds)
    pay[:, 0, :] = w * (1.0 - oy)
    pay[:, 1, :] = w * oy
    pay[:, 2, :] = 1.0 - os
    pay[:, 3, :] = os
    pay[:, 4, :] = (head * (cells * lines) + xy[...]).astype(jnp.float32)
    pay[:, 5, :] = (state - head * speeds).astype(jnp.float32)
    pay[:, 6, :] = jnp.zeros((groups, slots), jnp.float32)
    pay[:, 7, :] = jnp.zeros((groups, slots), jnp.float32)

    loads[6].wait()
    pl.semaphore_wait(barrier, groups - 1 + 2)

    def h_copy(side):
        return pltpu.make_async_remote_copy(
            value.at[0 if side == 0 else heads - 1], hhalo.at[1 - side],
            h_send.at[side], h_recv.at[1 - side],
            device_id=(me, h_prev if side == 0 else h_next), device_id_type=MESH,
        )

    def x_copy(side):
        return pltpu.make_async_remote_copy(
            value.at[:, 0 if side == 0 else cells - 1], xhalo.at[1 - side],
            x_send.at[side], x_recv.at[1 - side],
            device_id=(me - 1 if side == 0 else me + 1, hb), device_id_type=MESH,
        )

    def pay_copy(d):
        peer = lax.rem(me + d, groups)
        return pltpu.make_async_remote_copy(
            pay.at[peer], got.at[d], pay_send.at[d], pay_recv.at[d],
            device_id=(peer, hb), device_id_type=MESH,
        )

    for side in range(2):
        h_copy(side).start()
    for side, has in ((0, has_prev), (1, has_next)):
        @pl.when(has)
        def _():
            x_copy(side).start()

    if groups <= 8:
        for d in range(groups - 1, 0, -1):
            pay_copy(d).start()
    else:
        pl.loop(1, groups)(lambda d: pay_copy(d).start())
    mine = pltpu.make_async_copy(pay.at[me], got.at[0], self_sem)
    mine.start()
    loads[7].wait()

    for side, has in ((0, has_prev), (1, has_next)):
        @pl.when(jnp.logical_not(has))
        def _():
            xhalo[side] = value[:, 0 if side == 0 else cells - 1]

    total = heads * blocks
    angles = [np.float32(2.0 * math.pi / total) * np.float32(k) for k in range(total)]
    cosines = [float(np.cos(a)) for a in angles]
    sines = [float(np.sin(a)) for a in angles]
    speed = SLOWEST + SPEED_RANGE * lax.broadcasted_iota(jnp.int32, (1, speeds), 1).astype(
        jnp.float32
    ) / (speeds - 1)
    cx = [pick(cosines, hb * heads + h) * speed for h in range(heads)]
    cy = [pick(sines, hb * heads + h) * speed for h in range(heads)]
    grid = [(h, x) for h in range(heads) for x in range(cells)]
    v = {(h, x): value[h, x] for h, x in grid}
    part, s_slope = {}, {}
    for h, x in grid:
        here = v[h, x]
        up, down = upper(here, 0), lower(here, 0)
        term = cy[h] * (up - down) * 0.5 - (up - 2.0 * here + down) * 0.5
        up, down = upper(here, 1), lower(here, 1)
        slope = 0.5 * (up - down)
        size = smooth_abs(slope)
        s_slope[h, x] = slope / size
        part[h, x] = term + ACCELERATION * size - ACCELERATION * 0.5 * (up - 2.0 * here + down)

    for side in range(2):
        h_copy(side).wait_recv()
    for side, has in ((0, has_prev), (1, has_next)):
        @pl.when(has)
        def _():
            x_copy(1 - side).wait_recv()
    for x in range(cells):
        v[-1, x] = hhalo[0, x]
        v[heads, x] = hhalo[1, x]
    for h in range(heads):
        v[h, -1] = xhalo[0, h]
        v[h, cells] = xhalo[1, h]

    share, h_slope, above = {}, {}, {}
    for h, x in grid:
        here = v[h, x]
        up, down = v[h + 1, x], v[h - 1, x]
        slope = 0.5 * (up - down)
        size = smooth_abs(slope)
        h_slope[h, x] = slope / size
        turning = TURN_RATE * size - TURN_RATE * 0.5 * (up - 2.0 * here + down)
        up, down = v[h, x + 1], v[h, x - 1]
        across = cx[h] * (up - down) * 0.5 - (up - 2.0 * here + down) * 0.5
        relaxed = here - TIME_STEP * (across + part[h, x] + turning)
        floor = avoid[h, x]
        excess = SHARPNESS * (relaxed - floor)
        small = jnp.exp(-jnp.abs(excess))
        share[h, x] = jnp.where(excess >= 0.0, 1.0, small) / (1.0 + small)
        above[h, x] = (excess, small)

    rows = heads * cells * lines
    row_id = lax.broadcasted_iota(jnp.int32, (rows, slots), 0).astype(jnp.float32)
    speed_id = lax.broadcasted_iota(jnp.int32, (speeds, slots), 0).astype(jnp.float32)

    def operands(d):
        one = got[d]
        cell = jnp.broadcast_to(one[4:5], (rows, slots))
        left = jnp.where(row_id == cell, one[0:1], jnp.where(row_id == cell + 1.0, one[1:2], 0.0))
        cell = jnp.broadcast_to(one[5:6], (speeds, slots))
        right = jnp.where(
            speed_id == cell, one[2:3], jnp.where(speed_id == cell + 1.0, one[3:4], 0.0)
        )
        return left, right

    def product(left, right):
        return lax.dot_general(
            left, right, (((1,), (1,)), ((), ())),
            precision=lax.Precision.HIGHEST, preferred_element_type=jnp.float32,
        )

    mine.wait()
    if groups <= 8:
        for d in range(1, groups):
            pay_copy(d).wait_recv()
        both = [operands(d) for d in range(groups)]
        deposit = product(
            jnp.concatenate([b[0] for b in both], 1), jnp.concatenate([b[1] for b in both], 1)
        )
    else:
        pl.loop(1, groups)(lambda d: pay_copy(d).wait_recv())
        deposit = lax.fori_loop(
            0, groups, lambda d, so_far: so_far + product(*operands(d)),
            jnp.zeros((rows, speeds), jnp.float32),
        )

    c, adj = {}, {}
    for n, (h, x) in enumerate(grid):
        adjoint = deposit[n * lines : (n + 1) * lines]
        c[h, x] = adjoint * share[h, x]
        carried[h, x] = c[h, x]
        adj[h, x] = adjoint
    def cx_copy(side):
        return pltpu.make_async_remote_copy(
            carried.at[:, 0 if side == 0 else cells - 1], cxhalo.at[1 - side],
            cx_send.at[side], cx_recv.at[1 - side],
            device_id=(me - 1 if side == 0 else me + 1, hb), device_id_type=MESH,
        )

    for side, has in ((0, has_prev), (1, has_next)):
        @pl.when(has)
        def _():
            cx_copy(side).start()

        @pl.when(jnp.logical_not(has))
        def _():
            cxhalo[side] = jnp.zeros_like(cxhalo[side])
    ahead, back = {}, {}
    for h, x in grid:
        pull = (0.5 * TURN_RATE) * c[h, x] * h_slope[h, x]
        keep = (0.5 * TURN_RATE) * c[h, x]
        ahead[h, x] = pull - keep
        back[h, x] = -pull - keep
    for x in range(cells):
        turned[0, x] = back[0, x]
        turned[1, x] = ahead[heads - 1, x]

    def ch_copy(side):
        return pltpu.make_async_remote_copy(
            turned.at[side], chhalo.at[1 - side], ch_send.at[side], ch_recv.at[1 - side],
            device_id=(me, h_prev if side == 0 else h_next), device_id_type=MESH,
        )

    for side in range(2):
        ch_copy(side).start()

    local = {}
    for h, x in grid:
        excess, small = above[h, x]
        next_o[h, x] = avoid[h, x] + (jnp.maximum(excess, 0.0) + jnp.log1p(small)) / SHARPNESS
        agrad_o[h, x] = adj[h, x] * (jnp.where(excess >= 0.0, small, 1.0) / (1.0 + small))
        here = c[h, x]
        grad = spread((0.5 * cy[h] - 0.5) * here, (-0.5 * cy[h] - 0.5) * here, 0)
        pull = (0.5 * ACCELERATION) * here * s_slope[h, x]
        keep = (0.5 * ACCELERATION) * here
        grad = grad + spread(pull - keep, -pull - keep, 1)
        local[h, x] = grad + (2.0 + TURN_RATE + ACCELERATION) * here

    for side in range(2):
        ch_copy(side).wait_recv()
    for side, has in ((0, has_prev), (1, has_next)):
        @pl.when(has)
        def _():
            cx_copy(1 - side).wait_recv()
    for h, x in grid:
        grad = local[h, x]
        grad = grad + (ahead[h - 1, x] if h > 0 else chhalo[0, x])
        grad = grad + (back[h + 1, x] if h < heads - 1 else chhalo[1, x])
        low, high = 0.5 * cx[h] - 0.5, -0.5 * cx[h] - 0.5
        if x > 0:
            grad = grad + low * c[h, x - 1]
        else:
            grad = grad + jnp.where(has_prev, low * cxhalo[0, h], high * c[h, x])
        if x < cells - 1:
            grad = grad + high * c[h, x + 1]
        else:
            grad = grad + jnp.where(has_next, high * cxhalo[1, h], low * c[h, x])
        vgrad_o[h, x] = c[h, x] - TIME_STEP * grad

    for side in range(2):
        h_copy(side).wait_send()
        ch_copy(side).wait_send()
    for side, has in ((0, has_prev), (1, has_next)):
        @pl.when(has)
        def _():
            x_copy(side).wait_send()
            cx_copy(side).wait_send()
    if groups <= 8:
        for d in range(1, groups):
            pay_copy(d).wait_send()
    else:
        pl.loop(1, groups)(lambda d: pay_copy(d).wait_send())


def write_out(next_v, vgrad_v, agrad_v, next_o, vgrad_o, agrad_o, sem):
    copies = [
        pltpu.make_async_copy(a, b, sem.at[i])
        for i, (a, b) in enumerate(((next_v, next_o), (vgrad_v, vgrad_o), (agrad_v, agrad_o)))
    ]
    for copy in copies:
        copy.start()
    for copy in copies:
        copy.wait()


def on_device(groups, blocks, value, avoid, weight, offy, offs, xy, hs, count):
    slots = weight.shape[3]
    value = jnp.transpose(value, (0, 2, 3, 1))
    avoid = jnp.transpose(avoid, (0, 2, 3, 1))
    weight, offy, offs, xy, hs = (a.reshape(groups, slots) for a in (weight, offy, offs, xy, hs))
    count = count.reshape(1, groups)
    heads, cells, lines, speeds = value.shape
    f32 = jnp.float32
    dma = pltpu.SemaphoreType.DMA
    field = pltpu.VMEM(value.shape, f32)
    x_pair = pltpu.VMEM((2, heads, lines, speeds), f32)
    h_pair = pltpu.VMEM((2, cells, lines, speeds), f32)
    outs = pl.pallas_call(
        functools.partial(kernel, groups, blocks),
        out_shape=[pltpu.VMEM(value.shape, f32)] * 3,
        in_specs=[pl.BlockSpec(memory_space=pltpu.HBM)] * 8,
        out_specs=[pl.BlockSpec(memory_space=pltpu.VMEM)] * 3,
        scratch_shapes=[
            field, field,
            *[pltpu.VMEM((groups, slots), f32)] * 3,
            *[pltpu.VMEM((groups, slots), jnp.int32)] * 2,
            pltpu.VMEM((1, groups), jnp.int32),
            pltpu.VMEM((groups, ROWS, slots), f32), pltpu.VMEM((groups, ROWS, slots), f32),
            x_pair, h_pair, field, h_pair, x_pair, h_pair,
            dma((8,)), dma((groups,)), dma((groups,)),
            dma((2,)), dma((2,)), dma((2,)), dma((2,)),
            dma((2,)), dma((2,)), dma((2,)), dma((2,)), dma,
        ],
        compiler_params=pltpu.CompilerParams(collective_id=0, has_side_effects=True),
        name="step",
    )(value, avoid, weight, offy, offs, xy, hs, count)
    outs = pl.pallas_call(
        write_out,
        out_shape=[jax.ShapeDtypeStruct(value.shape, f32)] * 3,
        in_specs=[pl.BlockSpec(memory_space=pl.ANY)] * 3,
        out_specs=[pl.BlockSpec(memory_space=pl.ANY)] * 3,
        scratch_shapes=[dma((3,))],
        compiler_params=pltpu.CompilerParams(vmem_limit_bytes=1 << 20),
        name="write_out",
    )(*outs)
    return tuple(jnp.transpose(o, (0, 3, 1, 2)) for o in outs)


def solution(mesh):
    field = P("ha", None, "gx", None)
    sample = P("gx", "ha", None, None)
    return jax.shard_map(
        functools.partial(on_device, mesh.shape["gx"], mesh.shape["ha"]),
        mesh=mesh,
        in_specs=(field, field, sample, sample, sample, sample, sample, P("gx", "ha", None)),
        out_specs=(field, field, field),
        check_vma=False,
    )
```
